256 devices in a mesh: dp: 16 (over z, core), tensor: 4 (over y), section: 4 (over x).
Axes of the slice: x: 4, y: 4, z: 8, core: 2. Of those that a mesh axis runs over, the one named last changes fastest.
Arguments:
- grads: bfloat16 [16, 64, 768, 768], P('dp', 'section', 'tensor'), may hold values from -1 to 1
- owner: int32 [64, 1], P('section'), may hold values from 0 to 15; in each aligned block of 16 rows (0 to 15, 16 to 31, ...) at most 2 rows name the same one
- left_stat: float32 [16, 4, 2, 768, 768], P('dp', 'section', None, 'tensor')
- right_stat: float32 [16, 4, 2, 768, 768], P('dp', 'section', None, 'tensor')
- second_moment: float32 [16, 4, 2, 768, 768], P('dp', 'section', None, 'tensor'), may hold values from 0.05 to 4.5
- left_root: bfloat16 [16, 4, 2, 768, 768], P('dp', 'section', None, 'tensor')
- right_root: bfloat16 [16, 4, 2, 768, 768], P('dp', 'section', None, 'tensor')
Outputs:
- left_new: float32 [16, 4, 2, 768, 768], P('dp', 'section', None, 'tensor')
- right_new: float32 [16, 4, 2, 768, 768], P('dp', 'section', None, 'tensor')
- second_new: float32 [16, 4, 2, 768, 768], P('dp', 'section', None, 'tensor')
- direction: bfloat16 [16, 4, 2, 768, 768], P('dp', 'section', None, 'tensor')
The draws below stay inside these ranges and needn't reach their ends.
Inputs may be any that keep to these rules, and one draw needn't show every extreme that they name: `owner`: among the 16 blocks of one section, no dp rank owns more than 2.
All inputs are finite; a program needn't handle non-finite values.
Results may differ from the reference program's by a relative error of at most 0.02.
Values may be sent and summed in bfloat16 or wider, within the bound.
No kernel may reach another device: no remote copies, remote signals or barrier semaphores. Data moves between devices by JAX's collectives and lax.ppermute only.
A program may use at most 128 MiB of HBM per device.

```python
import math
import jax
import jax.numpy as jnp
import numpy as np
from jax import lax

WIDTH = 768
CAP = 2
BLK_ST = 16
NB = 64
N_DP = 16
N_TENSOR = 4
N_SECTION = 4


def block_factor(key, low, high):
    shape = (N_DP, N_SECTION, CAP, N_TENSOR)
    values = jnp.exp(jax.random.uniform(key, shape, jnp.float32, math.log(low), math.log(high)))
    return jnp.repeat(values, WIDTH // N_TENSOR, axis=-1)


def symmetric_block(key, diag_low, diag_high, off_scale, rising):
    shape = (N_DP, N_SECTION, CAP, WIDTH, WIDTH)
    first_key, second_key = jax.random.split(key)
    noise = jax.random.normal(first_key, shape, jnp.float32) * off_scale
    noise = (noise + jnp.swapaxes(noise, -1, -2)) * 0.70710678
    diag_vals = jnp.exp(jax.random.uniform(second_key, shape[:-1], jnp.float32, math.log(diag_low), math.log(diag_high)))
    if rising:
        diag_vals = diag_vals * block_factor(jax.random.fold_in(key, 21), 1.0, 3.0)
    on_diag = jnp.arange(WIDTH)[:, None] == jnp.arange(WIDTH)[None, :]
    return jnp.where(on_diag, diag_vals[..., :, None], noise)


def draw_left_stat(key, part):
    return symmetric_block(jax.random.fold_in(key, 11), 4.0, 40.0, 0.5, False)


def draw_right_stat(key, part):
    return symmetric_block(jax.random.fold_in(key, 12), 4.0, 40.0, 0.5, False)


def draw_left_root(key, part):
    return symmetric_block(jax.random.fold_in(key, 13), 0.25, 0.35, 0.01, True).astype(jnp.bfloat16)


def draw_right_root(key, part):
    return symmetric_block(jax.random.fold_in(key, 14), 0.25, 0.35, 0.01, True).astype(jnp.bfloat16)


def draw_second_moment(key, part):
    shape = (N_DP, N_SECTION, CAP, WIDTH, WIDTH)
    inner = jax.random.fold_in(key, 15)
    base = jnp.exp(jax.random.uniform(inner, shape, jnp.float32, math.log(0.05), math.log(0.5)))
    factor = block_factor(jax.random.fold_in(key, 16), 1.0, 9.0)
    return base * factor[..., :, None]


def spiked(values, own_key, source, target, shards_of, factor):
    owner, partner = [(jnp.arange(values.shape[dim]) // (values.shape[dim] // shards_of)).reshape([-1 if axis == dim else 1 for axis in range(values.ndim)]) for dim in (source, target)]
    chosen = jax.random.permutation(own_key, shards_of)[partner]
    strong = (owner == chosen) | (owner == (partner + shards_of // 2) % shards_of)
    return jnp.where(strong, factor * values, values)


def block_scale(own_key, extent, cuts, low, largest):
    loudness, own = 1.0, jax.random.fold_in(own_key, 6)
    for position, shards_of in cuts:
        heights = jnp.exp(jax.random.uniform(jax.random.fold_in(own, position), (shards_of,), jnp.float32, low / len(cuts), largest / len(cuts)))
        loudness = loudness * jnp.repeat(heights, extent[position] // shards_of).reshape([-1 if axis == position else 1 for axis in range(len(extent))])
    return loudness


def deal_out(stream_key, own, number, rows, count, top, limit, slope):
    sequence = jax.random.permutation(stream_key, count)
    heavy_load, ordinary = shares(count, rows * top, limit, slope, True), shares(count, rows * top, limit, slope, False)
    places = jnp.arange(count)

    def named(lengths, turn):
        used = int((lengths > 0).sum())
        fixed = max(1, used // 4)
        moved = fixed + (places - fixed + turn * (used - fixed)) % max(1, count - fixed)
        return jnp.zeros((count,), jnp.int32).at[sequence[jnp.where(places < fixed, places, moved)]].set(jnp.asarray(lengths, jnp.int32))

    lengths = jnp.where(number % 4 == 0, named(heavy_load, number // 4), named(ordinary, number - number // 4 - 1))
    mixed = jax.random.permutation(jax.random.fold_in(own, 3), count)
    giver, receiver = mixed[0:count // 2 * 2:2], mixed[1:count // 2 * 2:2]
    margin = jnp.minimum(lengths[giver] - 1, limit - lengths[receiver]) // 2
    margin = jnp.where((giver == sequence[0]) | (receiver == sequence[0]) | (lengths[receiver] == 0), 0, jnp.maximum(margin, 0))
    moved = jax.random.randint(jax.random.fold_in(own, 4), (count // 2,), 0, 1 << 20) % (margin + 1)
    lengths = lengths.at[giver].add(-moved).at[receiver].add(moved)
    items = jnp.searchsorted(jnp.cumsum(lengths), jnp.arange(rows * top), side="right").astype(jnp.int32)
    table = items.reshape(top, rows).T
    table = table[jax.random.permutation(jax.random.fold_in(own, 1), rows)]
    turn = jax.random.randint(jax.random.fold_in(own, 2), (rows, 1), 0, top)
    return jnp.take_along_axis(table, (jnp.arange(top)[None, :] + turn) % top, axis=1)


def shares(count, total, bound, skew, full):
    portions = [(1 << 20) // math.isqrt(grade ** skew) + 1 for grade in range(1, count + 1)]
    largest = bound if full else min(bound, max(-(-total // count), total * portions[0] // sum(portions)))
    least = 1 if total - largest >= count - 1 else 0
    holding, surplus = [largest] + [least] * (count - 1), total - largest - least * (count - 1)
    while surplus > 0:
        free = [i for i in range(1, count) if holding[i] < largest] or [i for i in range(1, count) if holding[i] < bound]
        whole, budget = sum([portions[i] for i in free]), surplus
        for i in free:
            addition = min(bound - holding[i], max(1, budget * portions[i] // whole), surplus)
            holding[i] = holding[i] + addition
            surplus = surplus - addition
    return np.array(holding)


def gaussian_with(rng, extent, width, reach, pieces, heavy, held_as=jnp.bfloat16):
    result = width * jax.random.normal(rng, extent, jnp.float32)
    if pieces:
        result = result * block_scale(rng, extent, pieces, -0.22, 0.18)
    return jnp.clip(spiked(result, jax.random.fold_in(rng, 3), *heavy), -reach, reach).astype(held_as)


def setup_inputs(seed: int = 0) -> dict:
    key_of = jax.random.split(jax.random.key(seed), 8)
    grads = gaussian_with(key_of[0], (N_DP, NB, WIDTH, WIDTH), (0.5 / N_DP ** 0.5), 1.0, ((0, 16), (1, 4), (2, 4)), (0, 1, 16, 2.0))
    owner_keys = jax.random.split(jax.random.fold_in(key_of[1], 1), NB // BLK_ST)
    owner_turns = jax.random.permutation(jax.random.fold_in(key_of[1], 3), NB // BLK_ST)
    owner = jax.vmap(lambda own, number: deal_out(jax.random.fold_in(key_of[1], 2), own, number, BLK_ST, N_DP, 1, CAP, 2))(owner_keys, owner_turns).reshape((NB, 1))
    left_stat = draw_left_stat(jax.random.fold_in(key_of[7], 71), 0)
    right_stat = draw_right_stat(jax.random.fold_in(key_of[7], 71), 0)
    second_moment = draw_second_moment(jax.random.fold_in(key_of[7], 71), 0)
    left_root = draw_left_root(jax.random.fold_in(key_of[7], 71), 0)
    right_root = draw_right_root(jax.random.fold_in(key_of[7], 71), 0)
    return {"grads": grads, "owner": owner, "left_stat": left_stat, "right_stat": right_stat, "second_moment": second_moment, "left_root": left_root, "right_root": right_root}


def slot_index(owner):
    owners_grid = owner[:, 0].reshape(N_SECTION, BLK_ST)
    positions = jnp.arange(BLK_ST, dtype=jnp.int32)
    same_owner = owners_grid[:, :, None] == owners_grid[:, None, :]
    earlier = positions[None, :] < positions[:, None]
    ranked = lax.optimization_barrier(jnp.sum((same_owner & earlier[None]).astype(jnp.int32), axis=2))
    ranks_dp = jnp.arange(N_DP, dtype=jnp.int32)
    slot_ids = jnp.arange(CAP, dtype=jnp.int32)
    chosen = (owners_grid[None, :, None, :] == ranks_dp[:, None, None, None]) & (ranked[None, :, None, :] == slot_ids[None, None, :, None])
    local_pos = lax.optimization_barrier(jnp.sum(chosen.astype(jnp.int32) * positions[None, None, None, :], axis=3))
    section_base = (jnp.arange(N_SECTION, dtype=jnp.int32) * BLK_ST)[None, :, None]
    return ((local_pos + section_base).astype(jnp.int32), jnp.any(chosen, axis=3))

def one_slot(inputs):
    gradient, left_stat, right_stat, second_moment, left_root, right_root = inputs
    grad_wide = gradient.astype(jnp.float32)
    left_new = 0.95 * left_stat + 0.05 * jnp.dot(gradient, gradient.T, preferred_element_type=jnp.float32)
    right_new = 0.95 * right_stat + 0.05 * jnp.dot(gradient.T, gradient, preferred_element_type=jnp.float32)
    second_new = 0.9 * second_moment + 0.1 * grad_wide * grad_wide
    adam_dir = grad_wide / (jnp.sqrt(second_new) + 1e-08)
    mixed = jnp.dot(left_root, gradient, preferred_element_type=jnp.float32).astype(jnp.bfloat16)
    precond = jnp.dot(mixed, right_root, preferred_element_type=jnp.float32)
    scaling = jnp.sqrt(jnp.sum(adam_dir * adam_dir)) / jnp.sqrt(jnp.sum(precond * precond) + 1e-06)
    direction = (precond * scaling).astype(jnp.bfloat16)
    return (left_new, right_new, second_new, direction)

def reference(grads, owner, left_stat, right_stat, second_moment, left_root, right_root):

    def accumulate(total, replica):
        return (total + replica.astype(jnp.float32), None)
    summed, unused = lax.scan(accumulate, jnp.zeros((NB, WIDTH, WIDTH), jnp.float32), grads)
    index_table, occupied = slot_index(owner)
    slot_sum = jnp.take(summed, index_table.reshape(-1), axis=0)
    slot_sum = slot_sum * occupied.reshape(-1)[:, None, None].astype(jnp.float32)
    gradient = slot_sum.astype(jnp.bfloat16)
    count = N_DP * N_SECTION * CAP
    flat = (gradient, left_stat.reshape(count, WIDTH, WIDTH), right_stat.reshape(count, WIDTH, WIDTH), second_moment.reshape(count, WIDTH, WIDTH), left_root.reshape(count, WIDTH, WIDTH), right_root.reshape(count, WIDTH, WIDTH))
    left_new, right_new, second_new, direction = lax.map(one_slot, flat)
    shape = (N_DP, N_SECTION, CAP, WIDTH, WIDTH)
    return (left_new.reshape(shape), right_new.reshape(shape), second_new.reshape(shape), direction.reshape(shape))
```

```python
import functools

import jax
import jax.numpy as jnp
from jax import lax
from jax.experimental import pallas as pl
from jax.experimental.pallas import tpu as pltpu
from jax.sharding import PartitionSpec as P

CAP = 2
F32 = jnp.float32
BF16 = jnp.bfloat16
OFFSETS = (4, 3, -3, 2, -2, 1, -1, 0)


def z_shift(chips, shift):
    return [(z * 2 + k, ((z + shift) % chips) * 2 + k) for z in range(chips) for k in range(2)]


def y_shift(count, shift):
    return [(i, (i + shift) % count) for i in range(count)]


def partner(count):
    return [(i, i ^ 1) for i in range(count)]


def slot_table(owner, ranks):
    owners = owner[:, 0]
    positions = jnp.arange(owners.shape[0], dtype=jnp.int32)
    same = owners[:, None] == owners[None, :]
    earlier = positions[None, :] < positions[:, None]
    ranked = jnp.sum((same & earlier).astype(jnp.int32), axis=1)
    slots = jnp.arange(CAP, dtype=jnp.int32)
    chosen = (owners[None, None, :] == ranks[:, None, None]) & (
        ranked[None, None, :] == slots[None, :, None]
    )
    index = jnp.sum(chosen.astype(jnp.int32) * positions, axis=2).reshape(-1)
    valid = jnp.sum(chosen.astype(jnp.int32), axis=2).reshape(-1)
    return jnp.concatenate([index, valid])


def call(body, name, grid, in_specs, out_specs, out_shape, args, table=None, scratch=()):
    spec = pltpu.PrefetchScalarGridSpec(
        num_scalar_prefetch=1,
        grid=grid,
        in_specs=in_specs,
        out_specs=out_specs,
        scratch_shapes=list(scratch),
    )
    return pl.pallas_call(
        body,
        grid_spec=spec,
        out_shape=out_shape,
        name=name,
        compiler_params=pltpu.CompilerParams(
            dimension_semantics=("arbitrary",) * len(grid), vmem_limit_bytes=48 << 20
        ),
    )(table, *args)


def copy_body(tab, x, o):
    o[...] = x[0]


def load(ref):
    return ref[...].reshape(ref.shape[-2:]).astype(F32)


def first_body(tab, gp, gm, qp, qm, op, om, *, valid):
    keep = tab[valid] > 0
    op[...] = jnp.where(keep, load(gp) + load(qp), 0.0).astype(BF16)
    om[...] = jnp.where(keep, load(gm) + load(qm), 0.0).astype(BF16)


def round_body(tab, gp, gm, qp, qm, rp, rm, op, om, *, vp, vm, half):
    g = pl.program_id(0)
    plus = jnp.where(tab[vp] > 0, load(gp) + load(qp), 0.0)
    minus = jnp.where(tab[vm] > 0, load(gm) + load(qm), 0.0)
    if half:
        plus += jnp.where(g == 0, load(rp), 0.0)
        minus += jnp.where(g == 1, load(rm), 0.0)
    else:
        plus += load(rp)
        minus += load(rm)
    op[...] = plus.astype(BF16)
    om[...] = minus.astype(BF16)


def last_body(tab, g0, q0, rp, rm, o, *, valid):
    own = jnp.where(tab[valid] > 0, load(g0) + load(q0), 0.0)
    o[...] = (own + load(rp) + load(rm)).astype(BF16)


def assemble(tab, dst, pieces, rows, parts):
    y = tab[36]
    for shift, piece in pieces:
        at = lax.rem(y + shift, parts) * rows
        dst[pl.ds(pl.multiple_of(at, 16), rows), :] = piece[...].reshape(rows, dst.shape[1])


def precond_body(tab, g0, gl, gr, g2, r0, rl, rr, r2, left, o, acc, gf, rf, *, rows, parts):
    assemble(tab, gf, ((0, g0), (parts - 1, gl), (1, gr), (2, g2)), rows, parts)
    assemble(tab, rf, ((0, r0), (parts - 1, rl), (1, rr), (2, r2)), rows, parts)
    mixed = jnp.dot(
        left[...].reshape(rows, gf.shape[0]), gf[...], preferred_element_type=F32
    ).astype(BF16)
    pre = jnp.dot(mixed, rf[...], preferred_element_type=F32)
    o[...] = pre
    acc[...] = jnp.broadcast_to(jnp.sum(pre * pre), acc.shape)


def stats_body(tab, g0, gl, gr, g2, ls, rs, ln, rn, gf, *, rows, parts):
    assemble(tab, gf, ((0, g0), (parts - 1, gl), (1, gr), (2, g2)), rows, parts)
    whole = gf[...]
    nt = (((1,), (1,)), ((), ()))
    incr = lax.dot_general(g0[...], whole, nt, preferred_element_type=F32)
    ln[...] = 0.95 * ls[...].reshape(ln.shape) + 0.05 * incr
    width = gf.shape[1]
    at = lax.broadcasted_iota(jnp.int32, (rows, width), 0) + tab[36] * rows
    pick = (lax.broadcasted_iota(jnp.int32, (rows, width), 1) == at).astype(BF16)
    mine = lax.dot_general(pick, whole, nt, preferred_element_type=F32).astype(BF16)
    incr = jnp.dot(mine, whole, preferred_element_type=F32)
    rn[...] = 0.95 * rs[...].reshape(rn.shape) + 0.05 * incr


def scale_body(tab, p0, p1, s0, s1, s2, s3, o):
    j = pl.program_id(0)
    total = s0[...] + s1[...] + s2[...] + s3[...]
    adam, pre = total[0], total[1]
    scale = jnp.sqrt(adam) / jnp.sqrt(pre + 1e-06)
    value = jnp.where(j == 0, p0[...], p1[...])
    o[...] = (value * scale[0:1, 0:1]).astype(BF16).reshape(o.shape)


def per_device(chips, parts, grads, owner, left_stat, right_stat, second, left_root, right_root):
    ranks_count = chips * 2
    blocks, rows, width = grads.shape[1:]
    half = rows // 2
    me = lax.axis_index("dp")
    y = lax.axis_index("tensor").astype(jnp.int32)
    z, core = me // 2, me % 2
    ranks = jnp.stack(
        [lax.rem(z + o + chips, chips) * 2 + core for o in OFFSETS]
        + [lax.rem(z + 4, chips) * 2 + 1 - core]
    ).astype(jnp.int32)
    table = jnp.concatenate([slot_table(owner, ranks), y[None]])
    NV = 2 * 9

    def sds(*shape, dtype=BF16):
        return jax.ShapeDtypeStruct(shape, dtype)

    def blk(entry, h, rank4=True):
        return pl.BlockSpec((1, 1, half, width), lambda g, t: (0, t[entry], h(g), 0))

    def perm(x, axis, pairs, scope):
        with jax.named_scope(scope):
            return lax.ppermute(x, axis, pairs)

    zp, zm = z_shift(chips, 1), z_shift(chips, -1)
    swap = partner(ranks_count)
    with jax.named_scope("k0"):
        early = call(
            copy_body, "k0", (CAP,),
            [pl.BlockSpec((1, 1, rows, width), lambda g, t: (0, t[16 + g], 0, 0))],
            pl.BlockSpec((1, rows, width), lambda g, t: (g, 0, 0)),
            sds(CAP, rows, width), (grads,), table,
        )
    early = perm(early, "dp", swap, "p0")
    other = perm(grads, "dp", swap, "p1")

    state = []
    for j in range(CAP):
        with jax.named_scope(f"k1{j}"):
            p, m = call(
                functools.partial(first_body, valid=NV + j), f"k1{j}", (1,),
                [blk(j, lambda g: 0), blk(j, lambda g: 1),
                 pl.BlockSpec((1, half, width), lambda g, t, j=j: (j, 0, 0)),
                 pl.BlockSpec((1, half, width), lambda g, t, j=j: (j, 1, 0))],
                [pl.BlockSpec((half, width), lambda g, t: (0, 0))] * 2,
                [sds(half, width)] * 2, (grads, grads, early, early), table,
            )
        p = perm(p, "dp", zp, f"c{j}r1p")
        m = perm(m, "dp", zm, f"c{j}r1m")
        state.append((p, m))
    roots = right_root[0, 0]
    r_l = perm(roots, "tensor", y_shift(parts, 1), "rl")
    r_r = perm(roots, "tensor", y_shift(parts, -1), "rr")
    r_2 = perm(roots, "tensor", y_shift(parts, 2), "r2")

    here = lambda g: g
    row_spec = pl.BlockSpec((half, width), lambda g, t: (g, 0))
    fixed = pl.BlockSpec((half, width), lambda g, t: (0, 0))
    for rnd in (2, 3, 4):
        a, b = 2 * rnd - 3, 2 * rnd - 2
        for j in range(CAP):
            p, m = state[j]
            first = rnd == 2
            ep, em = a * CAP + j, b * CAP + j
            with jax.named_scope(f"k{rnd}{j}"):
                p, m = call(
                    functools.partial(round_body, vp=NV + ep, vm=NV + em, half=first),
                    f"k{rnd}{j}", (2,),
                    [blk(ep, here), blk(em, here), blk(ep, here), blk(em, here),
                     fixed if first else row_spec, fixed if first else row_spec],
                    [row_spec] * 2, [sds(rows, width)] * 2,
                    (grads, grads, other, other, p, m), table,
                )
            p = perm(p, "dp", zp, f"c{j}r{rnd}p")
            m = perm(m, "dp", zm, f"c{j}r{rnd}m")
            state[j] = (p, m)

    full = pl.BlockSpec((rows, width), lambda g, t: (0, 0))
    tile = pl.BlockSpec((8, 128), lambda g, t: (0, 0))

    def slot_spec(j, r=rows):
        return pl.BlockSpec((1, 1, 1, r, width), lambda g, t: (0, 0, j, g, 0))

    def stack_spec(j):
        return pl.BlockSpec((1, rows, width), lambda g, t: (j, 0, 0))

    grad, gathered, second_new, adam = [], [], [], []
    for j in range(CAP):
        p, m = state[j]
        e = 7 * CAP + j
        with jax.named_scope(f"k5{j}"):
            g = call(
                functools.partial(last_body, valid=NV + e), f"k5{j}", (2,),
                [blk(e, here), blk(e, here), row_spec, row_spec],
                row_spec, sds(rows, width), (grads, other, p, m), table,
            )
        grad.append(g)
        g_l = perm(g, "tensor", y_shift(parts, 1), f"g{j}l")
        g_r = perm(g, "tensor", y_shift(parts, -1), f"g{j}r")
        g_2 = perm(g, "tensor", y_shift(parts, 2), f"g{j}2")
        gathered.append((g, g_l, g_r, g_2))
        with jax.named_scope(f"s{j}"):
            new, acc = call(
                second_body, f"s{j}", (2,),
                [row_spec, slot_spec(j, half)],
                [row_spec, tile], [sds(rows, width, dtype=F32), sds(8, 128, dtype=F32)],
                (g, second), table,
            )
        second_new.append(new)
        adam.append(acc)

    pre, pre_sq, left_new, right_new = [], [], [], []
    scratch = pltpu.VMEM((width, width), BF16)
    for j in range(CAP):
        with jax.named_scope(f"f{j}"):
            o, acc = call(
                functools.partial(precond_body, rows=rows, parts=parts), f"f{j}", (1,),
                [full] * 4 + [stack_spec(j)] * 4 + [slot_spec(j)],
                [full, tile], [sds(rows, width, dtype=F32), sds(8, 128, dtype=F32)],
                (*gathered[j], roots, r_l, r_r, r_2, left_root), table, (scratch, scratch),
            )
        pre.append(o)
        pre_sq.append(acc)
    sums = jnp.stack([jnp.stack([adam[j], pre_sq[j]]) for j in range(CAP)])
    s_l = perm(sums, "tensor", y_shift(parts, 1), "nl")
    s_r = perm(sums, "tensor", y_shift(parts, -1), "nr")
    s_2 = perm(sums, "tensor", y_shift(parts, 2), "n2")
    for j in range(CAP):
        with jax.named_scope(f"t{j}"):
            ln, rn = call(
                functools.partial(stats_body, rows=rows, parts=parts), f"t{j}", (1,),
                [full] * 4 + [slot_spec(j)] * 2,
                [full, full], [sds(rows, width, dtype=F32)] * 2,
                (*gathered[j], left_stat, right_stat), table, (scratch,),
            )
        left_new.append(ln)
        right_new.append(rn)
    sum_spec = pl.BlockSpec((pl.squeezed, 2, 8, 128), lambda g, t: (g, 0, 0, 0))
    with jax.named_scope("scale"):
        direction = call(
            scale_body, "scale", (CAP,),
            [full, full] + [sum_spec] * 4,
            pl.BlockSpec((1, 1, 1, rows, width), lambda g, t: (0, 0, g, 0, 0)),
            sds(1, 1, CAP, rows, width), (*pre, sums, s_l, s_r, s_2), table,
        )
    join = lambda parts_: jnp.stack(parts_)[None, None]
    return join(left_new), join(right_new), join(second_new), direction


def second_body(tab, g, s, o, acc):
    wide = g[...].astype(F32)
    new = 0.9 * s[...].reshape(o.shape) + 0.1 * wide * wide
    o[...] = new
    adam = wide / (jnp.sqrt(new) + 1e-08)

    @pl.when(pl.program_id(0) == 0)
    def _():
        acc[...] = jnp.zeros_like(acc)

    acc[...] += jnp.broadcast_to(jnp.sum(adam * adam), acc.shape)


def solution(mesh):
    sharded = P("dp", "section", None, "tensor", None)
    placed = (P("dp", "section", "tensor", None), P("section", None)) + (sharded,) * 5
    chips, parts = mesh.shape["dp"] // 2, mesh.shape["tensor"]
    return jax.shard_map(
        functools.partial(per_device, chips, parts),
        mesh=mesh,
        in_specs=placed,
        out_specs=(sharded,) * 4,
        check_vma=False,
    )
```

```python
import functools

import jax
import jax.numpy as jnp
from jax import lax
from jax.experimental import pallas as pl
from jax.experimental.pallas import tpu as pltpu
from jax.sharding import PartitionSpec as P


CAP = 2
F32 = jnp.float32
BF16 = jnp.bfloat16
OFFSETS = (4, 3, -3, 2, -2, 1, -1, 0)


def z_shift(chips, shift):
    return [(z * 2 + k, ((z + shift) % chips) * 2 + k) for z in range(chips) for k in range(2)]


def y_shift(count, shift):
    return [(i, (i + shift) % count) for i in range(count)]


def partner(count):
    return [(i, i ^ 1) for i in range(count)]


def slot_table(owner, ranks):
    owners = owner[:, 0]
    count = owners.shape[0]
    hit = owners[None, :] == ranks[:, None]
    at = lax.broadcasted_iota(jnp.int32, hit.shape, 1)
    first = jnp.min(jnp.where(hit, at, count - 1), axis=1)
    last = jnp.max(jnp.where(hit, at, 0), axis=1)
    hits = jnp.sum(hit.astype(jnp.int32), axis=1)
    return jnp.concatenate([first, last, (hits > 0).astype(jnp.int32), (hits > 1).astype(jnp.int32)])


def call(body, grid, in_specs, out_specs, out_shape, table, args, scratch=(), into=None):
    spec = pltpu.PrefetchScalarGridSpec(
        num_scalar_prefetch=1,
        grid=grid,
        in_specs=list(in_specs) + [pl.BlockSpec(memory_space=pl.ANY)] * len(into or ()),
        out_specs=out_specs,
        scratch_shapes=list(scratch),
    )
    skip = len(in_specs)

    def kernel(tab, *refs):
        body(tab, *refs[:skip], *refs[skip + len(into or ()):])

    aliases = {1 + skip + k: o for k, (o, _) in enumerate(into or ())}
    return pl.pallas_call(
        kernel,
        grid_spec=spec,
        out_shape=out_shape,
        input_output_aliases=aliases,
        compiler_params=pltpu.CompilerParams(
            dimension_semantics=("arbitrary",) * len(grid), vmem_limit_bytes=48 << 20
        ),
    )(table, *args, *[a for _, a in into or ()])


def copy_body(tab, x, o):
    o[...] = x[0]


def load(ref):
    return ref[...].reshape(ref.shape[-2:]).astype(F32)


def first_body(tab, gp, gm, qp, qm, op, om, *, valid):
    keep = tab[valid] > 0
    op[...] = jnp.where(keep, load(gp) + load(qp), 0.0).astype(BF16)
    om[...] = jnp.where(keep, load(gm) + load(qm), 0.0).astype(BF16)


def round_body(tab, gp, gm, qp, qm, rp, rm, op, om, *, vp, vm):
    plus = jnp.where(tab[vp] > 0, load(gp) + load(qp), 0.0)
    minus = jnp.where(tab[vm] > 0, load(gm) + load(qm), 0.0)
    half = rp.shape[0]
    if half < op.shape[0]:
        op[:half] = (plus[:half] + load(rp)).astype(BF16)
        op[half:] = plus[half:].astype(BF16)
        om[:half] = minus[:half].astype(BF16)
        om[half:] = (minus[half:] + load(rm)).astype(BF16)
    else:
        op[...] = (plus + load(rp)).astype(BF16)
        om[...] = (minus + load(rm)).astype(BF16)


def last_body(tab, g0, q0, rp, rm, o, *, valid):
    own = jnp.where(tab[valid] > 0, load(g0) + load(q0), 0.0)
    o[...] = (own + load(rp) + load(rm)).astype(BF16)


def gather_rows(dst, tab, own, left, right, far_a, far_b, rows, parts):
    y = tab[36]

    def put(shift, offset, piece):
        size = piece.shape[-2]
        at = lax.rem(y + shift, parts) * rows + offset
        dst[pl.ds(pl.multiple_of(at, 16), size), :] = piece[...].reshape(size, dst.shape[1])

    put(0, 0, own)
    put(parts - 1, 0, left)
    put(1, 0, right)
    put(2, 0, far_a)
    if far_b is not None:
        put(2, rows // 2, far_b)


def precond_body(
    tab, g0, gl, gr, ga, gb, r0, rl, rr, r2, left, adam, o, acc, gf, rf, *, rows, parts
):
    gather_rows(gf, tab, g0, gl, gr, ga, gb, rows, parts)
    gather_rows(rf, tab, r0, rl, rr, r2, None, rows, parts)
    mixed = jnp.dot(
        left[...].reshape(rows, gf.shape[0]), gf[...], preferred_element_type=F32
    ).astype(BF16)
    pre = jnp.dot(mixed, rf[...], preferred_element_type=F32)
    o[...] = pre
    acc[:8] = adam[...]
    acc[8:] = jnp.broadcast_to(jnp.sum(pre * pre), adam.shape)


def stats_body(tab, g0, gl, gr, ga, gb, ls, rs, ln, rn, gf, *, rows, parts):
    gather_rows(gf, tab, g0, gl, gr, ga, gb, rows, parts)
    whole = gf[...]
    nt = (((1,), (1,)), ((), ()))
    incr = lax.dot_general(g0[...], whole, nt, preferred_element_type=F32)
    ln[...] = 0.95 * ls[...] + (0.05 * incr).reshape(ln.shape)
    width = gf.shape[1]
    at = lax.broadcasted_iota(jnp.int32, (rows, width), 0) + tab[36] * rows
    pick = (lax.broadcasted_iota(jnp.int32, (rows, width), 1) == at).astype(BF16)
    mine = lax.dot_general(pick, whole, nt, preferred_element_type=F32).astype(BF16)
    incr = jnp.dot(mine, whole, preferred_element_type=F32)
    rn[...] = 0.95 * rs[...] + (0.05 * incr).reshape(rn.shape)


def scale_body(tab, p, s0, s1, s2, s3, o):
    total = s0[...] + s1[...] + s2[...] + s3[...]
    scale = jnp.sqrt(total[0:1, 0:1]) / jnp.sqrt(total[8:9, 0:1] + 1e-06)
    o[...] = (p[...] * scale).astype(BF16).reshape(o.shape)


def second_body(tab, g, s, o, acc):
    wide = g[...].astype(F32)
    new = 0.9 * s[...].reshape(wide.shape) + 0.1 * wide * wide
    o[...] = new.reshape(o.shape)
    adam = wide / (jnp.sqrt(new) + 1e-08)
    acc[...] = jnp.broadcast_to(jnp.sum(adam * adam), acc.shape)


def per_device(chips, parts, grads, owner, left_stat, right_stat, second, left_root, right_root):
    return step(chips, parts, grads, owner, left_stat, right_stat, second, left_root, right_root)


def step(chips, parts, grads, owner, left_stat, right_stat, second, left_root, right_root):
    rows, width = grads.shape[2:]
    half = rows // 2
    me = lax.axis_index("dp").astype(jnp.int32)
    y = lax.axis_index("tensor").astype(jnp.int32)
    z, core = lax.shift_right_logical(me, 1), me & 1
    number = len(OFFSETS) + 1
    entry = lax.iota(jnp.int32, number)
    offset = jnp.zeros_like(entry)
    for k, o in enumerate(OFFSETS):
        offset = jnp.where(entry == k, o + chips, offset)
    offset = jnp.where(entry == number - 1, OFFSETS[0] + chips, offset)
    side = jnp.where(entry == number - 1, 1 - core, core)
    ranks = lax.rem(z + offset, chips) * 2 + side
    table = jnp.concatenate([slot_table(owner, ranks), y[None]])

    def at(k, j):
        return j * number + k

    def ok(k, j):
        return (CAP + j) * number + k

    def sds(*shape, dtype=BF16):
        return jax.ShapeDtypeStruct(shape, dtype)

    def blk(k, j, size=rows, h=0):
        return pl.BlockSpec((1, 1, size, width), lambda g, t: (0, t[at(k, j)], h, 0))

    full = pl.BlockSpec((rows, width), lambda g, t: (0, 0))
    halves = pl.BlockSpec((half, width), lambda g, t: (0, 0))
    tile = pl.BlockSpec((8, 128), lambda g, t: (0, 0))
    tiles = pl.BlockSpec((16, 128), lambda g, t: (0, 0))
    zp, zm = z_shift(chips, 1), z_shift(chips, -1)
    yp, ym, yf = y_shift(parts, 1), y_shift(parts, -1), y_shift(parts, 2)
    swap = partner(chips * 2)
    grads = pltpu.with_memory_space_constraint(grads, pltpu.HBM)

    early = call(
        copy_body, (CAP,),
        [pl.BlockSpec((1, 1, rows, width), lambda g, t: (0, t[g * number + number - 1], 0, 0))],
        pl.BlockSpec((1, rows, width), lambda g, t: (g, 0, 0)),
        sds(CAP, rows, width), table, (grads,),
    )
    early = lax.ppermute(early, "dp", swap)
    other = lax.ppermute(grads, "dp", swap)

    state = []
    for j in range(CAP):
        p, m = call(
            functools.partial(first_body, valid=ok(0, j)), (1,),
            [blk(0, j, half, 0), blk(0, j, half, 1),
             pl.BlockSpec((1, half, width), lambda g, t, j=j: (j, 0, 0)),
             pl.BlockSpec((1, half, width), lambda g, t, j=j: (j, 1, 0))],
            [halves] * 2, [sds(half, width)] * 2, table, (grads, grads, early, early),
        )
        state.append((lax.ppermute(p, "dp", zp), lax.ppermute(m, "dp", zm)))
    roots = right_root[0, 0]
    r_l = lax.ppermute(roots, "tensor", yp)
    r_r = lax.ppermute(roots, "tensor", ym)
    r_2 = lax.ppermute(roots, "tensor", yf)

    for rnd in (2, 3, 4):
        a, b = 2 * rnd - 3, 2 * rnd - 2
        for j in range(CAP):
            recv = halves if rnd == 2 else full
            p, m = call(
                functools.partial(round_body, vp=ok(a, j), vm=ok(b, j)), (1,),
                [blk(a, j), blk(b, j), blk(a, j), blk(b, j), recv, recv],
                [full] * 2, [sds(rows, width)] * 2, table,
                (grads, grads, other, other, *state[j]),
            )
            state[j] = (lax.ppermute(p, "dp", zp), lax.ppermute(m, "dp", zm))

    def slot_spec(j):
        return pl.BlockSpec((1, 1, 1, rows, width), lambda g, t: (0, 0, j, 0, 0))

    def stack_spec(j):
        return pl.BlockSpec((1, rows, width), lambda g, t: (j, 0, 0))

    big = sds(1, 1, CAP, rows, width, dtype=F32)
    small = sds(8, 128, dtype=F32)
    scratch = pltpu.VMEM((width, width), BF16)
    second_new = left_new = right_new = direction = None

    def keep(*arrays):
        return None if arrays[0] is None else tuple(enumerate(arrays))

    for j in range(CAP):
        own = call(
            functools.partial(last_body, valid=ok(7, j)), (1,),
            [blk(7, j), blk(7, j), full, full], full, sds(rows, width), table,
            (grads, other, *state[j]),
        )
        g_l = lax.ppermute(own, "tensor", yp)
        g_r = lax.ppermute(own, "tensor", ym)
        g_a = lax.ppermute(g_l[:half], "tensor", yp)
        g_b = lax.ppermute(g_r[half:], "tensor", ym)
        whole = (own, g_l, g_r, g_a, g_b)
        whole_specs = [full] * 3 + [halves] * 2
        second_new, adam = call(
            second_body, (1,), [full, slot_spec(j)], [slot_spec(j), tile],
            [big, small], table, (own, second), into=keep(second_new),
        )
        pre, sq = call(
            functools.partial(precond_body, rows=rows, parts=parts), (1,),
            whole_specs + [stack_spec(j)] * 4 + [slot_spec(j), tile], [full, tiles],
            [sds(rows, width, dtype=F32), sds(16, 128, dtype=F32)], table,
            (*whole, roots, r_l, r_r, r_2, left_root, adam), (scratch, scratch),
        )
        sq_l = lax.ppermute(sq, "tensor", yp)
        sq_r = lax.ppermute(sq, "tensor", ym)
        sq_2 = lax.ppermute(sq, "tensor", yf)
        left_new, right_new = call(
            functools.partial(stats_body, rows=rows, parts=parts), (1,),
            whole_specs + [slot_spec(j)] * 2, [slot_spec(j)] * 2, [big, big], table,
            (*whole, left_stat, right_stat), (scratch,), into=keep(left_new, right_new),
        )
        direction = call(
            scale_body, (1,), [full] + [tiles] * 4, slot_spec(j),
            sds(1, 1, CAP, rows, width), table,
            (pre, sq, sq_l, sq_r, sq_2), into=keep(direction),
        )
    return left_new, right_new, second_new, direction


def solution(mesh):
    sharded = P("dp", "section", None, "tensor", None)
    placed = (P("dp", "section", "tensor", None), P("section", None)) + (sharded,) * 5
    chips, parts = mesh.shape["dp"] // 2, mesh.shape["tensor"]
    return jax.shard_map(
        functools.partial(per_device, chips, parts),
        mesh=mesh,
        in_specs=placed,
        out_specs=(sharded,) * 4,
        check_vma=False,
    )
```

```python
import functools

import jax
import jax.numpy as jnp
from jax import lax
from jax.experimental import pallas as pl
from jax.experimental.pallas import tpu as pltpu
from jax.sharding import PartitionSpec as P


CAP = 2
F32 = jnp.float32
BF16 = jnp.bfloat16
CHAINS = ((0, 0), (0, 1), (1, 0), (1, 1))


def slot_table(owner, ranks):
    owners = owner[:, 0]
    count = owners.shape[0]
    hit = owners[None, :] == ranks[:, None]
    at = lax.broadcasted_iota(jnp.int32, hit.shape, 1)
    first = jnp.min(jnp.where(hit, at, count - 1), axis=1)
    last = jnp.max(jnp.where(hit, at, 0), axis=1)
    hits = jnp.sum(hit.astype(jnp.int32), axis=1)
    return jnp.concatenate([first, last, (hits > 0).astype(jnp.int32), (hits > 1).astype(jnp.int32)])


def call(body, grid, in_specs, out_specs, out_shape, table, args, scratch=(), into=None):
    spec = pltpu.PrefetchScalarGridSpec(
        num_scalar_prefetch=1,
        grid=grid,
        in_specs=list(in_specs) + [pl.BlockSpec(memory_space=pl.ANY)] * len(into or ()),
        out_specs=out_specs,
        scratch_shapes=list(scratch),
    )
    skip = len(in_specs)

    def kernel(tab, *refs):
        body(tab, *refs[:skip], *refs[skip + len(into or ()):])

    aliases = {1 + skip + k: o for k, (o, _) in enumerate(into or ())}
    return pl.pallas_call(
        kernel,
        grid_spec=spec,
        out_shape=out_shape,
        input_output_aliases=aliases,
        compiler_params=pltpu.CompilerParams(
            dimension_semantics=("arbitrary",) * len(grid), vmem_limit_bytes=16 << 20
        ),
    )(table, *args, *[a for _, a in into or ()])


def early_body(tab, g, out, sems, *, entry, other):
    half = out.shape[1]
    start = pl.multiple_of(tab[other] * half, 16)
    copies = [
        pltpu.make_async_copy(
            g.at[0, tab[entry(1 - r, j)], pl.ds(start, half)], out.at[c], sems.at[c]
        )
        for c, (j, r) in enumerate(CHAINS)
    ]
    for copy in copies:
        copy.start()
    for copy in copies:
        copy.wait()


def first_body(tab, g, q, o, *, chain, entry, valid, core):
    half = o.shape[0]
    begin = pl.multiple_of(tab[core] * half, 16)
    total = g[0, tab[entry], pl.ds(begin, half), :].astype(F32) + q[chain].astype(F32)
    o[...] = jnp.where(tab[valid] > 0, total, 0.0).astype(BF16)


def local_sum(tab, g, q, entry, valid):
    total = g[0, tab[entry]].astype(F32) + q[0, tab[entry]].astype(F32)
    return jnp.where(tab[valid] > 0, total, 0.0)


def round_body(tab, g, q, r, o, *, entry, valid, core):
    total = local_sum(tab, g, q, entry, valid)
    got = r[...].astype(F32)
    half = r.shape[0]
    if half < o.shape[0]:
        o[:half] = (total[:half] + jnp.where(tab[core] == 0, got, 0.0)).astype(BF16)
        o[half:] = (total[half:] + jnp.where(tab[core] == 1, got, 0.0)).astype(BF16)
    else:
        o[...] = (total + got).astype(BF16)


def last_body(tab, g, q, r, p, o, *, entry, valid):
    total = local_sum(tab, g, q, entry, valid)
    o[...] = (total + (r[...].astype(F32) + p[...].astype(F32))).astype(BF16)


def second_body(tab, g, s, o, acc):
    wide = g[...].astype(F32)
    new = 0.9 * s[...].reshape(wide.shape) + 0.1 * wide * wide
    o[...] = new.reshape(o.shape)
    adam = wide / (jnp.sqrt(new) + 1e-08)
    acc[...] = jnp.broadcast_to(jnp.sum(adam * adam), acc.shape)


def put(dst, shard, rows, offset, piece, parts):
    size = piece.shape[-2]
    at = lax.rem(shard, parts) * rows + offset
    dst[pl.ds(pl.multiple_of(at, 16), size), :] = piece[...].reshape(size, dst.shape[1])


def root_body(tab, r0, rl, rr, r2, o, *, rows, parts, where):
    for j in range(CAP):
        for shift, piece in ((0, r0), (parts - 1, rl), (1, rr), (2, r2)):
            put(o.at[j], tab[where] + shift, rows, 0, piece[j], parts)


def precond_body(
    tab, own, near, handed, passed, adam, root, left, o, gf, acc, *, slot, rows, parts, where
):
    y, core = tab[where], tab[where + 1]
    ahead = 1 + core * (parts - 2)
    for shift, piece in ((0, own), (parts - ahead, near), (ahead, handed), (2, passed)):
        put(gf, y + shift, rows, 0, piece[...], parts)
    mixed = jnp.dot(
        left[...].reshape(rows, gf.shape[0]), gf[...], preferred_element_type=F32
    ).astype(BF16)
    pre = jnp.dot(mixed, root[slot], preferred_element_type=F32)
    o[...] = pre
    acc[:8] = adam[...]
    acc[8:] = jnp.broadcast_to(jnp.sum(pre * pre), adam.shape)


NT = (((1,), (1,)), ((), ()))


def stats_body(tab, gf, ls, rs, ln, rn, *, rows, where):
    whole = gf[...]
    own = gf[pl.ds(pl.multiple_of(tab[where] * rows, 16), rows), :]
    incr = lax.dot_general(own, whole, NT, preferred_element_type=F32)
    ln[...] = 0.95 * ls[...] + (0.05 * incr).reshape(ln.shape)
    width = whole.shape[1]
    at = lax.broadcasted_iota(jnp.int32, (rows, width), 0) + tab[where] * rows
    pick = (lax.broadcasted_iota(jnp.int32, (rows, width), 1) == at).astype(BF16)
    mine = lax.dot_general(pick, whole, NT, preferred_element_type=F32).astype(BF16)
    incr = jnp.dot(mine, whole, preferred_element_type=F32)
    rn[...] = 0.95 * rs[...] + (0.05 * incr).reshape(rn.shape)


def scale_body(tab, p0, p1, s, w, o):
    def run(j, p):
        total = s[j] + w[j]
        scale = jnp.sqrt(total[0:1, 0:1]) / jnp.sqrt(total[8:9, 0:1] + 1e-06)
        o[0, 0, 0] = (p[...] * scale).astype(BF16)

    for j, p in enumerate((p0, p1)):
        pl.when(pl.program_id(0) == j)(functools.partial(run, j, p))


def per_device(chips, parts, grads, owner, left_stat, right_stat, second, left_root, right_root):
    return step(chips, parts, grads, owner, left_stat, right_stat, second, left_root, right_root)


def step(chips, parts, grads, owner, left_stat, right_stat, second, left_root, right_root):
    rows, width = grads.shape[2:]
    me = lax.axis_index("dp").astype(jnp.int32)
    y = lax.axis_index("tensor").astype(jnp.int32)
    z, core = lax.shift_right_logical(me, 1), me & 1
    turn = 1 - 2 * core
    far = chips // 2
    number = 2 * (far + 1)
    entry = lax.iota(jnp.int32, number)
    away = far - lax.shift_right_logical(entry, 1)
    ranks = lax.rem(z + turn * away + chips, chips) * 2 + (core ^ 1 ^ (entry & 1))
    table = jnp.concatenate([slot_table(owner, ranks), jnp.stack([y, core, 1 - core])])
    where = 2 * CAP * number

    def at(k, r, j):
        return j * number + (far - k) * 2 + r

    def ok(k, r, j):
        return CAP * number + at(k, r, j)

    def sds(*shape, dtype=BF16):
        return jax.ShapeDtypeStruct(shape, dtype)

    ranks_all = [(a, k) for a in range(chips) for k in range(2)]
    step_z = [(a * 2 + k, (a + 1 - 2 * k) % chips * 2 + k) for a, k in ranks_all]
    swap = [(a * 2 + k, a * 2 + 1 - k) for a, k in ranks_all]
    both = ("dp", "tensor")
    step_y = [
        ((a * 2 + k) * parts + b, (a * 2 + k) * parts + (b + 1 - 2 * k) % parts)
        for a, k in ranks_all for b in range(parts)
    ]

    near_spec = pl.BlockSpec(memory_space=pltpu.VMEM)
    hbm = pltpu.with_memory_space_constraint(grads, pltpu.HBM)
    half = rows // 2

    early = call(
        functools.partial(early_body, entry=functools.partial(at, far), other=where + 2),
        (), [pl.BlockSpec(memory_space=pltpu.HBM)], near_spec,
        sds(len(CHAINS), half, width), table, (hbm,),
        (pltpu.SemaphoreType.DMA((len(CHAINS),)),),
    )
    early = lax.ppermute(early, "dp", swap)
    other = lax.ppermute(hbm, "dp", swap)
    other = pltpu.with_memory_space_constraint(other, pltpu.VMEM)
    grads = pltpu.with_memory_space_constraint(grads, pltpu.VMEM)

    state = []
    for c, (j, r) in enumerate(CHAINS):
        p = call(
            functools.partial(
                first_body, chain=c, entry=at(far, r, j), valid=ok(far, r, j), core=where + 1
            ),
            (), [near_spec] * 2, near_spec, sds(half, width), table, (grads, early),
        )
        state.append(lax.ppermute(p, "dp", step_z))
    roots = right_root[0, 0]
    shift_y = lambda s: [(b, (b + s) % parts) for b in range(parts)]
    r_l = lax.ppermute(roots, "tensor", shift_y(1))
    r_r = lax.ppermute(roots, "tensor", shift_y(-1))
    r_2 = lax.ppermute(roots, "tensor", shift_y(2))

    for rnd in range(2, far + 1):
        k = far + 1 - rnd
        for c, (j, r) in enumerate(CHAINS):
            p = call(
                functools.partial(
                    round_body, entry=at(k, r, j), valid=ok(k, r, j), core=where + 1
                ),
                (), [near_spec] * 3, near_spec, sds(rows, width), table,
                (grads, other, state[c]),
            )
            state[c] = lax.ppermute(p, "dp", step_z)

    def slot_spec(j):
        return pl.BlockSpec((1, 1, 1, rows, width), lambda g, t: (0, 0, j, 0, 0))

    tile = pl.BlockSpec((8, 128), lambda g, t: (0, 0))
    tiles = pl.BlockSpec((16, 128), lambda g, t: (0, 0))
    big = sds(1, 1, CAP, rows, width, dtype=F32)
    small = sds(8, 128, dtype=F32)
    second_new = left_new = right_new = None

    def keep(*arrays):
        return None if arrays[0] is None else tuple(enumerate(arrays))

    met = [lax.ppermute(state[c], "dp", swap) for c in range(len(CHAINS))]
    near, grad = [None] * len(CHAINS), [None] * len(CHAINS)
    for c in (1, 0, 3, 2):
        j, r = CHAINS[c]
        grad[c] = call(
            functools.partial(last_body, entry=at(0, r, j), valid=ok(0, r, j)),
            (), [near_spec] * 4, near_spec, sds(rows, width), table,
            (grads, other, state[c], met[c ^ 1]),
        )
        near[c] = lax.ppermute(grad[c], both, step_y)
    pieces, adam = [], []
    for j in range(CAP):
        c = 2 * j
        passed = lax.ppermute(near[c + 1], both, step_y)
        handed = lax.ppermute(near[c], "dp", swap)
        pieces.append((grad[c + 1], near[c + 1], handed, passed))
        second_new, acc = call(
            second_body, (1,), [near_spec, slot_spec(j)], [slot_spec(j), tile],
            [big, small], table, (grad[c + 1], second), into=keep(second_new),
        )
        adam.append(acc)

    roots = call(
        functools.partial(root_body, rows=rows, parts=parts, where=where), (),
        [near_spec] * 4, near_spec, sds(CAP, width, width), table, (roots, r_l, r_r, r_2),
    )
    pre, sums, whole = [], [], []
    for j in range(CAP):
        o, w, acc = call(
            functools.partial(precond_body, slot=j, rows=rows, parts=parts, where=where),
            (1,), [near_spec] * 4 + [tile, near_spec, slot_spec(j)],
            [near_spec, near_spec, tiles],
            [sds(rows, width, dtype=F32), sds(width, width), sds(16, 128, dtype=F32)], table,
            (*pieces[j], adam[j], roots, left_root),
        )
        pre.append(o)
        whole.append(w)
        sums.append(acc)
    sums = jnp.stack(sums)
    swapped = lax.ppermute(sums, "tensor", [(b, b ^ 1) for b in range(parts)])
    sums = sums + swapped
    swapped = lax.ppermute(sums, "tensor", [(b, b ^ 3) for b in range(parts)])
    for j in range(CAP):
        left_new, right_new = call(
            functools.partial(stats_body, rows=rows, where=where), (1,),
            [near_spec] + [slot_spec(j)] * 2, [slot_spec(j)] * 2, [big, big], table,
            (whole[j], left_stat, right_stat), into=keep(left_new, right_new),
        )
    both_slots = pl.BlockSpec((1, 1, 1, rows, width), lambda g, t: (0, 0, g, 0, 0))
    direction = call(
        scale_body, (CAP,), [near_spec] * 4, both_slots,
        sds(1, 1, CAP, rows, width), table, (*pre, sums, swapped),
    )
    return left_new, right_new, second_new, direction


def solution(mesh):
    sharded = P("dp", "section", None, "tensor", None)
    placed = (P("dp", "section", "tensor", None), P("section", None)) + (sharded,) * 5
    chips, parts = mesh.shape["dp"] // 2, mesh.shape["tensor"]
    return jax.shard_map(
        functools.partial(per_device, chips, parts),
        mesh=mesh,
        in_specs=placed,
        out_specs=(sharded,) * 4,
        check_vma=False,
    )
```
